128 devices in a mesh: sec: 2 (over core), dev: 64 (over z, x, y).
Axes of the slice: x: 4, y: 4, z: 4, core: 2. Of those that a mesh axis runs over, the one named last changes fastest.
Arguments:
- queries: bfloat16 [1024, 8192], P('dev', 'sec'), may hold values from -160 to 160
- key_cache: bfloat16 [1024, 768, 512], P('dev', None, 'sec'), may hold values from -5 to 5
- value_cache: bfloat16 [1024, 768, 512], P('dev', None, 'sec'), may hold values from -6 to 6
- new_key: bfloat16 [1024, 512], P('dev', 'sec'), may hold values from -4 to 4
- new_value: bfloat16 [1024, 512], P('dev', 'sec'), may hold values from -6 to 6
- cache_lengths: int32 [1024], P('dev'), may hold values from 1 to 768, 393216 in all
- residual_in: bfloat16 [1024, 4096], P('dev'), may hold values from -14 to 14
- out_weight: bfloat16 [8192, 4096], P('sec', 'dev'), may hold values from -0.5 to 0.5
- norm_gain: float32 [4096], replicated, may hold values from 0.1 to 1.9
- router_weight: bfloat16 [4096, 64], replicated, may hold values from -8 to 8
- expert_ids: int32 [1024, 8], P('dev'), may hold values from 0 to 63, all different within a row; in each aligned block of 16 rows (0 to 15, 16 to 31, ...) at most 4 rows name the same one
- gate_weight: bfloat16 [64, 4096, 768], P('dev', None, 'sec'), may hold values from -0.09375 to 0.09375
- up_weight: bfloat16 [64, 4096, 768], P('dev', None, 'sec'), may hold values from -0.09375 to 0.09375
- down_weight: bfloat16 [64, 768, 4096], P('dev', 'sec'), may hold values from -0.625 to 0.625
Outputs:
- layer_out: bfloat16 [1024, 4096], P('dev')
The draws below stay inside these ranges and needn't reach their ends.
Inputs may be any that keep to these rules, and one draw needn't show every extreme that they name: `cache_lengths`: the longest row has exactly 768 filled slots. `expert_ids`: in each aligned block of 16 rows (the rows of one chip) no expert is named by more than 4 rows, a bound that some block reaches.
All inputs are finite; a program needn't handle non-finite values. No bound on the sum of `cache_lengths` on one device may be relied on, other than what follows from the above.
Results may differ from the reference program's by a relative error of at most 0.012.
Values may be sent and summed in bfloat16 or wider, within the bound.
A program may use at most 128 MiB of HBM per device.

```python
import math
import jax
import jax.numpy as jnp
import numpy as np
from jax import lax

D = 4096
HEADS = 64
KV_HEADS = 4
HEAD = 128
FFW = 768
TOPK = 8
ROW_DEV = 16
CACHE = 768
EXPERTS = 64
ROWS = 1024
CAP = 4
N_DEV = 64


def base_new_key(key):
    return jnp.clip(jax.random.normal(jax.random.fold_in(key, 11), (ROWS, KV_HEADS * HEAD), jnp.float32), -4.0, 4.0)


def draw_new_key(key, part):
    return base_new_key(key).astype(jnp.bfloat16)


def draw_queries(key, part):
    values = jnp.clip(jax.random.normal(jax.random.fold_in(key, 12), (ROWS, HEADS * HEAD), jnp.float32), -6.0, 6.0)
    return values.astype(jnp.bfloat16)


def draw_key_cache(key, part):
    values = jnp.clip(jax.random.normal(jax.random.fold_in(key, 14), (ROWS, CACHE, KV_HEADS * HEAD), jnp.float32), -5.0, 5.0)
    return values.astype(jnp.bfloat16)


def draw_residual_in(key, part):
    noise = 0.5 * jnp.clip(jax.random.normal(jax.random.fold_in(key, 16), (ROWS, D), jnp.float32), -3.0, 3.0)
    row_scale = jnp.exp(jax.random.uniform(jax.random.fold_in(key, 18), (ROWS, 1), jnp.float32, math.log(0.3), math.log(3.0)))
    col_scale = jnp.exp(jax.random.uniform(jax.random.fold_in(key, 19), (1, D), jnp.float32, math.log(0.3), math.log(3.0)))
    return (noise * row_scale * col_scale).astype(jnp.bfloat16)


def draw_router_weight(key, part):
    values = jnp.clip(jax.random.normal(jax.random.fold_in(key, 21), (D, EXPERTS), jnp.float32), -4.0, 4.0) * (1.5 / math.sqrt(D))
    return values.astype(jnp.bfloat16)


def level_of(stream_key, extent, pieces, smallest, largest):
    factor_of = 1.0
    for axis_at, shards_of in pieces:
        steps = jax.random.uniform(jax.random.fold_in(jax.random.fold_in(stream_key, 6), axis_at), (shards_of,), jnp.float32, smallest / len(pieces), largest / len(pieces))
        factor_of = factor_of * jnp.repeat(jnp.exp(steps), extent[axis_at] // shards_of).reshape((-1,) + (1,) * (len(extent) - 1 - axis_at))
    return factor_of


def length_profile(amount, total, bound, lean):
    portions = [(1 << 20) // math.isqrt(standing ** lean) + 1 for standing in range(2, amount + 1)]
    surplus, counts = total - bound - (amount - 1), [1] * (amount - 1)
    while surplus > 0:
        candidates = [i for i in range(amount - 1) if counts[i] < bound]
        whole, remaining = sum([portions[i] for i in candidates]), surplus
        for i in candidates:
            extra = min(bound - counts[i], max(1, remaining * portions[i] // whole), surplus)
            counts[i] = counts[i] + extra
            surplus = surplus - extra
    return np.array([bound] + counts)


def ragged(stream_key, amount, total, limit, lean):
    if amount == 2:
        one = jax.random.randint(stream_key, (), max(1, total - limit), min(limit, total - 1) + 1)
        return jnp.stack([one, total - one])
    sizes = jnp.asarray(length_profile(amount, total, limit, lean), jnp.int32)
    twos = (amount - 1) // 2
    source_of, sink = sizes[1:1 + 2 * twos:2], sizes[2:2 + 2 * twos:2]
    room = jnp.minimum(source_of - 1, limit - sink)
    passed = jax.random.randint(jax.random.fold_in(stream_key, 1), (twos,), 0, 1 << 20) % (room + 1)
    sizes = sizes.at[1:1 + 2 * twos:2].set(source_of - passed).at[2:2 + 2 * twos:2].set(sink + passed)
    return sizes[jax.random.permutation(jax.random.fold_in(stream_key, 2), amount)]


def assign_block(own_key, own, number, rows, number_of, top, reach, lean):
    order = jax.random.permutation(own_key, number_of)
    crowded, common = shares(number_of, rows * top, reach, lean, True), shares(number_of, rows * top, reach, lean, False)
    places = jnp.arange(number_of)

    def named(tallies, offset_by):
        used = int((tallies > 0).sum())
        fixed = max(1, used // 4)
        passed = fixed + (places - fixed + offset_by * (used - fixed)) % max(1, number_of - fixed)
        return jnp.zeros((number_of,), jnp.int32).at[order[jnp.where(places < fixed, places, passed)]].set(jnp.asarray(tallies, jnp.int32))

    tallies = jnp.where(number % 4 == 0, named(crowded, number // 4), named(common, number - number // 4 - 1))
    mixed = jax.random.permutation(jax.random.fold_in(own, 3), number_of)
    donor, receiver = mixed[0:number_of // 2 * 2:2], mixed[1:number_of // 2 * 2:2]
    margin = jnp.minimum(tallies[donor] - 1, reach - tallies[receiver]) // 2
    margin = jnp.where((donor == order[0]) | (receiver == order[0]) | (tallies[receiver] == 0), 0, jnp.maximum(margin, 0))
    passed = jax.random.randint(jax.random.fold_in(own, 4), (number_of // 2,), 0, 1 << 20) % (margin + 1)
    tallies = tallies.at[donor].add(-passed).at[receiver].add(passed)
    labels = jnp.searchsorted(jnp.cumsum(tallies), jnp.arange(rows * top), side="right").astype(jnp.int32)
    table = labels.reshape(top, rows).T
    table = table[jax.random.permutation(jax.random.fold_in(own, 1), rows)]
    offset_by = jax.random.randint(jax.random.fold_in(own, 2), (rows, 1), 0, top)
    return jnp.take_along_axis(table, (jnp.arange(top)[None, :] + offset_by) % top, axis=1)


def shares(number_of, total, most, lean, full):
    weights = [(1 << 20) // math.isqrt(rank ** lean) + 1 for rank in range(1, number_of + 1)]
    largest = most if full else min(most, max(-(-total // number_of), total * weights[0] // sum(weights)))
    least = 1 if total - largest >= number_of - 1 else 0
    counts, surplus = [largest] + [least] * (number_of - 1), total - largest - least * (number_of - 1)
    while surplus > 0:
        candidates = [i for i in range(1, number_of) if counts[i] < largest] or [i for i in range(1, number_of) if counts[i] < most]
        whole, left = sum([weights[i] for i in candidates]), surplus
        for i in candidates:
            extra = min(most - counts[i], max(1, left * weights[i] // whole), surplus)
            counts[i] = counts[i] + extra
            surplus = surplus - extra
    return np.array(counts)


def scatter_about(key, shape, scale, most, cuts=(), held_as=jnp.bfloat16):
    result = scale * jax.random.normal(key, shape, jnp.float32)
    if cuts:
        result = result * level_of(key, shape, cuts, -0.22, 0.18)
    return jnp.clip(result, -most, most).astype(held_as)


def setup_inputs(seed: int = 0) -> dict:
    arg_keys = jax.random.split(jax.random.key(seed), 15)
    queries = draw_queries(jax.random.fold_in(arg_keys[14], 71), 0)
    key_cache = draw_key_cache(jax.random.fold_in(arg_keys[14], 71), 0)
    value_cache = scatter_about(arg_keys[2], (ROWS, CACHE, KV_HEADS * HEAD), 1.0, 6.0, ((0, 64), (2, 2)))
    new_key = draw_new_key(jax.random.fold_in(arg_keys[14], 71), 0)
    new_value = scatter_about(arg_keys[4], (ROWS, KV_HEADS * HEAD), 1.0, 6.0, ((0, 64), (1, 2)))
    cache_lengths = ragged(arg_keys[5], ROWS, ROWS * CACHE // 2, CACHE, 2).astype(jnp.int32)
    residual_in = draw_residual_in(jax.random.fold_in(arg_keys[14], 71), 0)
    out_weight = scatter_about(arg_keys[7], (HEADS * HEAD, D), (HEADS * HEAD // 64) ** -0.5, 0.5, ((0, 2), (1, 64)))
    norm_gain = jnp.clip(1.0 + 0.18 * jax.random.normal(arg_keys[8], (D,), jnp.float32), 0.1, 1.9)
    router_weight = draw_router_weight(jax.random.fold_in(arg_keys[14], 71), 0)
    expert_ids_keys = jax.random.split(jax.random.fold_in(arg_keys[10], 1), ROWS // ROW_DEV)
    expert_ids_turns = jax.random.permutation(jax.random.fold_in(arg_keys[10], 3), ROWS // ROW_DEV)
    expert_ids = jax.vmap(lambda own, number: assign_block(jax.random.fold_in(arg_keys[10], 2), own, number, ROW_DEV, EXPERTS, TOPK, CAP, 2))(expert_ids_keys, expert_ids_turns).reshape((ROWS, TOPK))
    gate_weight = scatter_about(arg_keys[11], (EXPERTS, D, FFW), D ** -0.5, 0.09375, ((0, 64), (2, 2)))
    up_weight = scatter_about(arg_keys[12], (EXPERTS, D, FFW), D ** -0.5, 0.09375, ((0, 64), (2, 2)))
    down_weight = scatter_about(arg_keys[13], (EXPERTS, FFW, D), (FFW // 8) ** -0.5, 0.625, ((0, 64), (1, 2)))
    return dict(queries=queries, key_cache=key_cache, value_cache=value_cache, new_key=new_key, new_value=new_value, cache_lengths=cache_lengths, residual_in=residual_in, out_weight=out_weight, norm_gain=norm_gain, router_weight=router_weight, expert_ids=expert_ids, gate_weight=gate_weight, up_weight=up_weight, down_weight=down_weight)


masked_score = -1e+30

def attend_rows(packed):
    query_rows, key_rows, value_rows, fresh_key, fresh_value, length_rows = packed
    block_rows = query_rows.shape[0]
    group_count = KV_HEADS
    per_group = HEADS // KV_HEADS
    score_scale = 1.0 / math.sqrt(HEAD)
    query_heads = query_rows.astype(jnp.float32).reshape(block_rows, group_count, per_group, HEAD)
    keys_f = key_rows.astype(jnp.float32).reshape(block_rows, CACHE, group_count, HEAD)
    values_f = value_rows.astype(jnp.float32).reshape(block_rows, CACHE, group_count, HEAD)
    scores = jnp.einsum('rgqh,rcgh->rgqc', query_heads, keys_f) * score_scale
    positions = jnp.arange(CACHE, dtype=jnp.int32)
    live_mask = positions[None, :] < length_rows[:, None]
    scores = jnp.where(live_mask[:, None, None, :], scores, masked_score)
    fresh_keys = fresh_key.astype(jnp.float32).reshape(block_rows, group_count, HEAD)
    fresh_score = jnp.einsum('rgqh,rgh->rgq', query_heads, fresh_keys) * score_scale
    row_max = jnp.maximum(lax.optimization_barrier(jnp.max(scores, axis=-1)), fresh_score)
    exp_cache = jnp.exp(scores - row_max[..., None])
    exp_fresh = jnp.exp(fresh_score - row_max)
    denominator = lax.optimization_barrier(jnp.sum(exp_cache, axis=-1)) + exp_fresh
    weights_bf = (exp_cache / denominator[..., None]).astype(jnp.bfloat16)
    fresh_weight = (exp_fresh / denominator).astype(jnp.bfloat16)
    attended = jnp.einsum('rgqc,rcgh->rgqh', weights_bf.astype(jnp.float32), values_f)
    fresh_values = fresh_value.astype(jnp.float32).reshape(block_rows, group_count, 1, HEAD)
    attended = attended + fresh_weight.astype(jnp.float32)[..., None] * fresh_values
    return attended.reshape(block_rows, HEADS * HEAD).astype(jnp.bfloat16)

def reference(queries, key_cache, value_cache, new_key, new_value, cache_lengths, residual_in, out_weight, norm_gain, router_weight, expert_ids, gate_weight, up_weight, down_weight):
    block_rows = math.gcd(ROWS, 64)
    block_total = ROWS // block_rows

    def split_rows(array):
        return array.reshape((block_total, block_rows) + array.shape[1:])
    packed = tuple((split_rows(array) for array in (queries, key_cache, value_cache, new_key, new_value, cache_lengths)))
    attended = lax.map(attend_rows, packed).reshape(ROWS, HEADS * HEAD)
    projected = jnp.dot(attended, out_weight, preferred_element_type=jnp.float32).astype(jnp.bfloat16)
    mixed = (residual_in.astype(jnp.float32) + projected.astype(jnp.float32)).astype(jnp.bfloat16)
    mixed_f = mixed.astype(jnp.float32)
    mean_square = lax.optimization_barrier(jnp.mean(mixed_f * mixed_f, axis=-1, keepdims=True))
    normed = (mixed_f * lax.rsqrt(mean_square + 1e-06) * norm_gain).astype(jnp.bfloat16)
    logits = jnp.dot(normed, router_weight, preferred_element_type=jnp.float32)
    chosen = jnp.take_along_axis(logits, expert_ids, axis=1)
    route_weights = jax.nn.softmax(chosen, axis=-1)
    pair_total = ROWS * TOPK
    flat_ids = expert_ids.reshape(pair_total)
    expert_hot = (flat_ids[:, None] == jnp.arange(EXPERTS, dtype=jnp.int32)[None, :]).astype(jnp.int32)
    rank = lax.optimization_barrier(jnp.sum((jnp.cumsum(expert_hot, axis=0) - expert_hot) * expert_hot, axis=1)).astype(jnp.int32)
    slot_total = N_DEV * CAP
    row_of_pair = (jnp.arange(pair_total, dtype=jnp.int32) // TOPK).astype(jnp.int32)
    table = jnp.zeros((EXPERTS, slot_total), jnp.int32).at[flat_ids, rank].set(row_of_pair)
    half_units = FFW // 2

    def run_expert(expert_pack):
        table_row, gate_e, up_e, down_e = expert_pack
        inputs_e = normed[table_row]
        gate_act = jnp.dot(inputs_e, gate_e, preferred_element_type=jnp.float32)
        up_act = jnp.dot(inputs_e, up_e, preferred_element_type=jnp.float32)
        hidden = (jax.nn.silu(gate_act) * up_act).astype(jnp.bfloat16)
        first_half = jnp.dot(hidden[:, :half_units], down_e[:half_units], preferred_element_type=jnp.float32).astype(jnp.bfloat16)
        second_half = jnp.dot(hidden[:, half_units:], down_e[half_units:], preferred_element_type=jnp.float32).astype(jnp.bfloat16)
        return (first_half, second_half)
    first_out, second_out = lax.map(run_expert, (table, gate_weight, up_weight, down_weight))
    picked = first_out[flat_ids, rank].astype(jnp.float32) + second_out[flat_ids, rank].astype(jnp.float32)
    weighted = picked * route_weights.reshape(pair_total)[:, None]
    contribution = lax.optimization_barrier(jnp.sum(weighted.reshape(ROWS, TOPK, D), axis=1))
    return (mixed.astype(jnp.float32) + contribution).astype(jnp.bfloat16)
```

```python
import math

import jax
import jax.numpy as jnp
from jax import lax
from jax.experimental import pallas as pl
from jax.experimental.pallas import tpu as pltpu
from jax.sharding import PartitionSpec as P

HEAD = 128
MESH = pl.DeviceIdType.MESH
VMEM = pl.BlockSpec(memory_space=pltpu.VMEM)
F32 = jnp.float32
BF16 = jnp.bfloat16

masked_score = -1e30


def landed(ref, sem):
    pltpu.make_async_copy(ref, ref, sem).wait()


def nt_dot(a, b):
    return lax.dot_general(a, b, (((1,), (1,)), ((), ())), preferred_element_type=F32)


def tn_dot(a, b):
    return lax.dot_general(a, b, (((0,), (0,)), ((), ())), preferred_element_type=F32)


def greet(s, me, n_dev):
    barrier = pltpu.get_barrier_semaphore()
    pl.semaphore_signal(barrier, inc=1, device_id=(1 - s, me), device_id_type=MESH)

    def body(i, carry):
        pl.semaphore_signal(
            barrier, inc=1, device_id=(s, lax.rem(me + i, n_dev)), device_id_type=MESH
        )
        return carry

    lax.fori_loop(1, n_dev, body, 0)


def met(n_dev):
    pl.semaphore_wait(pltpu.get_barrier_semaphore(), n_dev)


def remote(src, dst, send_sem, recv_sem, s, d):
    pltpu.make_async_remote_copy(
        src_ref=src,
        dst_ref=dst,
        send_sem=send_sem,
        recv_sem=recv_sem,
        device_id=(s, d),
        device_id_type=MESH,
    ).start()


def project_kernel(
    att, wt, res, out, wbuf, abuf, pown, psend, precv, rsend, rbuf,
    sw, rw, sa, ra, sx, rx, sr, rr, sm, rm,
):
    n_dev = 64
    s = lax.axis_index("sec")
    me = lax.axis_index("dev")
    group, part = me // 8, lax.rem(me, 8)
    plane = me // 16
    greet(s, me, n_dev)
    own_w = pltpu.make_async_copy(
        wt.at[:, pl.ds(pl.multiple_of(part * 512, 512), 512)],
        wbuf.at[pl.ds(pl.multiple_of(part * 64, 64), 64)],
        rw,
    )
    own_w.start()
    own_a = pltpu.make_async_copy(
        att.at[:, pl.ds(pl.multiple_of(part * 512, 512), 512)],
        abuf.at[pl.ds(pl.multiple_of(me * 16, 16), 16)],
        ra.at[plane],
    )
    own_a.start()
    met(n_dev)

    def send_w(i, carry):
        m = lax.rem(part + i, 8)
        remote(
            wt.at[:, pl.ds(pl.multiple_of(m * 512, 512), 512)],
            wbuf.at[pl.ds(pl.multiple_of(part * 64, 64), 64)],
            sw, rw, s, group * 8 + m,
        )
        return carry

    lax.fori_loop(1, 8, send_w, 0)

    def send_a(i, carry):
        d = lax.rem(me + i, n_dev)
        remote(
            att.at[:, pl.ds(pl.multiple_of(lax.rem(d, 8) * 512, 512), 512)],
            abuf.at[pl.ds(pl.multiple_of(me * 16, 16), 16)],
            sa, ra.at[plane], s, d,
        )
        return carry

    lax.fori_loop(1, n_dev, send_a, 0)
    landed(wbuf, rw)
    own_cols = pl.ds(pl.multiple_of(s * 256, 256), 256)
    other_cols = pl.ds(pl.multiple_of((1 - s) * 256, 256), 256)
    for i in range(4):
        p = lax.rem(plane + i, 4)
        rows = pl.ds(pl.multiple_of(p * 256, 256), 256)
        landed(abuf.at[rows], ra.at[p])
        psend[rows] = nt_dot(abuf[rows], wbuf[other_cols]).astype(BF16)
        remote(psend.at[rows], precv.at[rows], sx, rx.at[p], 1 - s, me)
        pown[rows] = nt_dot(abuf[rows], wbuf[own_cols])
    for i in range(4):
        p = lax.rem(plane + i, 4)
        rows = pl.ds(pl.multiple_of(p * 256, 256), 256)
        landed(precv.at[rows], rx.at[p])
        rsend[rows] = (pown[rows] + precv[rows].astype(F32)).astype(BF16)

        def send_r(t, carry):
            d = p * 16 + lax.rem(me + t, 16)
            src = rsend.at[pl.ds(pl.multiple_of(d * 16, 16), 16)]
            dst = rbuf.at[pl.ds(pl.multiple_of(me * 16, 16), 16)]
            if i == 0:

                @pl.when(t != 0)
                def _():
                    remote(src, dst, sr, rr, s, d)

                @pl.when(t == 0)
                def _():
                    pltpu.make_async_copy(src, dst, rr).start()
            else:
                remote(src, dst, sr, rr, s, d)
            return carry

        lax.fori_loop(0, 16, send_r, 0)
    landed(rbuf, rr)
    for j in range(8):
        total = rbuf[pl.ds(128 * j, 16)].astype(F32)
        for k in range(1, 8):
            total += rbuf[pl.ds(128 * j + 16 * k, 16)].astype(F32)
        cols = pl.ds(pl.multiple_of(512 * j + 256 * s, 256), 256)
        out[:, cols] = (
            res[:, cols].astype(F32) + total.astype(BF16).astype(F32)
        ).astype(BF16)
        remote(out.at[:, cols], out.at[:, cols], sm, rm, 1 - s, me)
    landed(rbuf.at[pl.ds(0, 128)], rm)
    landed(rbuf.at[pl.ds(0, 128)], sm)
    landed(wbuf.at[pl.ds(0, 448)], sw)
    landed(abuf.at[pl.ds(0, 1008)], sa)
    landed(psend, sx)
    landed(rbuf.at[pl.ds(0, 1008)], sr)


def project(attended, weight_t, residual):
    sems = pltpu.SemaphoreType.DMA
    return pl.pallas_call(
        project_kernel,
        out_shape=jax.ShapeDtypeStruct((16, 4096), BF16),
        in_specs=[VMEM] * 3,
        out_specs=VMEM,
        scratch_shapes=[
            pltpu.VMEM((512, 512), BF16),
            pltpu.VMEM((1024, 512), BF16),
            pltpu.VMEM((1024, 256), F32),
            pltpu.VMEM((1024, 256), BF16),
            pltpu.VMEM((1024, 256), BF16),
            pltpu.VMEM((1024, 256), BF16),
            pltpu.VMEM((1024, 256), BF16),
            sems, sems, sems, sems((4,)), sems, sems((4,)), sems, sems, sems, sems,
        ],
        compiler_params=pltpu.CompilerParams(
            collective_id=0, has_side_effects=True, vmem_limit_bytes=40 << 20
        ),
        name="project",
    )(attended, weight_t, residual)


def expert_kernel(
    mixed, gain, router_t, ids_t, gate, up, down, out,
    wgu, wd, normed, sbuf, xr, x, act, hid, yown, ysend, yrecv, rs, back, stack,
    lw, ss, rs_sem, sx, rx, sy, ry, sb, rb, so, ro,
):
    n_dev = 64
    s = lax.axis_index("sec")
    me = lax.axis_index("dev")
    plane = me // 16
    greet(s, me, n_dev)
    loads = [
        pltpu.make_async_copy(gate.at[0], wgu.at[:, pl.ds(0, 384)], lw.at[0]),
        pltpu.make_async_copy(up.at[0], wgu.at[:, pl.ds(384, 384)], lw.at[1]),
        pltpu.make_async_copy(down.at[0], wd, lw.at[2]),
    ]
    for load in loads:
        load.start()

    def own(j):
        return pl.ds(pl.multiple_of(512 * j + 256 * s, 256), 256)

    def other(j):
        return pl.ds(pl.multiple_of(512 * j + 256 * (1 - s), 256), 256)

    mixed_f = mixed[...].astype(F32)
    mean_square = jnp.mean(mixed_f * mixed_f, axis=-1, keepdims=True)
    normed[...] = (mixed_f * lax.rsqrt(mean_square + 1e-06) * gain[...]).astype(BF16)
    for q in range(4):
        stack[pl.ds(16 * q, 16), pl.ds(0, 256)] = normed[:, own(2 * q)]
        stack[pl.ds(16 * q, 16), pl.ds(256, 256)] = normed[:, own(2 * q + 1)]

    chosen_t = jnp.zeros((64, 16), F32)
    expert_row = lax.broadcasted_iota(jnp.int32, (64, 16), 0)
    for k in range(8):
        chosen_t += jnp.where(ids_t[pl.ds(k, 1), :] == expert_row, 1.0, 0.0)
    earlier = jnp.where(
        lax.broadcasted_iota(jnp.int32, (16, 16), 0) < lax.broadcasted_iota(jnp.int32, (16, 16), 1),
        1.0,
        0.0,
    ).astype(BF16)
    chosen_tb = chosen_t.astype(BF16)
    rank_tb = jnp.dot(chosen_tb, earlier, preferred_element_type=F32).astype(BF16)
    lane = lax.broadcasted_iota(jnp.int32, (64, 1024), 1)
    spread = jnp.where(
        lane // 16 == lax.broadcasted_iota(jnp.int32, (64, 1024), 0), 1.0, 0.0
    ).astype(BF16)
    chosen_x = tn_dot(chosen_tb, spread)
    rank_x = tn_dot(rank_tb, spread)
    lane16 = lax.broadcasted_iota(jnp.int32, (16, 1024), 1)
    slot_hot = jnp.where(
        rank_x == lax.rem(lane16, 4).astype(F32), chosen_x, 0.0
    )
    quarter = lax.rem(lane16 // 4, 4)
    placed = jnp.concatenate(
        [jnp.where(quarter == q, slot_hot, 0.0) for q in range(4)], axis=0
    )
    sbuf[...] = tn_dot(placed.astype(BF16), stack[...]).astype(BF16)
    pltpu.make_async_copy(
        sbuf.at[pl.ds(pl.multiple_of(me * 16, 16), 16)],
        xr.at[pl.ds(pl.multiple_of(me * 16, 16), 16)],
        rs_sem.at[plane],
    ).start()
    met(n_dev)

    def send_x(i, carry):
        d = lax.rem(me + i, n_dev)
        remote(
            sbuf.at[pl.ds(pl.multiple_of(d * 16, 16), 16)],
            xr.at[pl.ds(pl.multiple_of(me * 16, 16), 16)],
            ss, rs_sem.at[plane], s, d,
        )
        return carry

    lax.fori_loop(1, n_dev, send_x, 0)

    logits = nt_dot(normed[...], router_t[...])
    eye = jnp.where(
        lax.broadcasted_iota(jnp.int32, (64, 64), 0) == lax.broadcasted_iota(jnp.int32, (64, 64), 1),
        1.0,
        0.0,
    ).astype(BF16)
    chosen = tn_dot(chosen_tb, eye)
    masked = jnp.where(chosen > 0.5, logits, masked_score)
    top = jnp.max(masked, axis=-1, keepdims=True)
    raised = jnp.where(chosen > 0.5, jnp.exp(masked - top), 0.0)
    weights = raised / jnp.sum(raised, axis=-1, keepdims=True)
    high = weights.astype(BF16)
    low = (weights - high.astype(F32)).astype(BF16)
    high_x = jnp.dot(high, spread, preferred_element_type=F32)
    low_x = jnp.dot(low, spread, preferred_element_type=F32)

    row = lax.broadcasted_iota(jnp.int32, (256, 256), 0)
    col = lax.broadcasted_iota(jnp.int32, (256, 256), 1)
    source = (lax.rem(row, 64) // 4) * 16 + (row // 64) * 4 + lax.rem(row, 4)
    order = jnp.where(col == source, 1.0, 0.0).astype(BF16)

    for i in range(4):
        p = lax.rem(plane + i, 4)
        wide = pl.ds(pl.multiple_of(p * 256, 256), 256)
        rows = pl.ds(pl.multiple_of(p * 64, 64), 64)
        landed(xr.at[wide], rs_sem.at[p])
        y = jnp.dot(order, xr[wide], preferred_element_type=F32).astype(BF16)
        for q in range(4):
            x[rows, own(2 * q)] = y[64 * q : 64 * q + 64, :256]
            x[rows, own(2 * q + 1)] = y[64 * q : 64 * q + 64, 256:]
        for j in range(8):
            remote(x.at[rows, own(j)], x.at[rows, own(j)], sx, rx.at[p], 1 - s, me)
    for i in range(4):
        landed(xr.at[pl.ds(0, 256)], rx.at[i])
    for load in loads:
        load.wait()

    def gate_up(n, carry):
        cols = pl.ds(pl.multiple_of(n * 256, 256), 256)
        act[:, cols] = jnp.dot(x[...], wgu[:, cols], preferred_element_type=F32)
        return carry

    lax.fori_loop(0, 3, gate_up, 0)
    gated = act[:, pl.ds(0, 384)]
    hid[...] = (gated / (1.0 + jnp.exp(-gated)) * act[:, pl.ds(384, 384)]).astype(BF16)
    for j in range(8):
        ysend[j] = jnp.dot(hid[...], wd[:, other(j)], preferred_element_type=F32).astype(BF16)
        remote(ysend.at[j], yrecv.at[j], sy, ry.at[j], 1 - s, me)
    for j in range(8):
        yown[j] = jnp.dot(hid[...], wd[:, own(j)], preferred_element_type=F32)
    for j in range(8):
        landed(yrecv.at[j], ry.at[j])
    for i in range(4):
        p = lax.rem(plane + i, 4)
        wide = pl.ds(pl.multiple_of(p * 256, 256), 256)
        rows = pl.ds(pl.multiple_of(p * 64, 64), 64)
        parts = []
        for q in range(4):
            parts.append(
                jnp.concatenate(
                    [
                        (yown[j, rows] + yrecv[j, rows].astype(F32)).astype(BF16)
                        for j in (2 * q, 2 * q + 1)
                    ],
                    axis=1,
                )
            )
        rs[wide] = tn_dot(order, jnp.concatenate(parts, axis=0)).astype(BF16)

        def send_b(t, carry):
            d = p * 16 + lax.rem(me + t, 16)
            src = rs.at[pl.ds(pl.multiple_of(d * 16, 16), 16)]
            dst = back.at[pl.ds(pl.multiple_of(me * 16, 16), 16)]
            if i == 0:

                @pl.when(t != 0)
                def _():
                    remote(src, dst, sb, rb, s, d)

                @pl.when(t == 0)
                def _():
                    pltpu.make_async_copy(src, dst, rb).start()
            else:
                remote(src, dst, sb, rb, s, d)
            return carry

        lax.fori_loop(0, 16, send_b, 0)

    combine_high = (placed * jnp.concatenate([high_x] * 4, axis=0)).astype(BF16)
    combine_low = (placed * jnp.concatenate([low_x] * 4, axis=0)).astype(BF16)
    landed(back, rb)
    summed = jnp.dot(combine_high, back[...], preferred_element_type=F32)
    summed += jnp.dot(combine_low, back[...], preferred_element_type=F32)
    for q in range(4):
        for h in range(2):
            cols = own(2 * q + h)
            out[:, cols] = (
                mixed[:, cols].astype(F32)
                + summed[16 * q : 16 * q + 16, 256 * h : 256 * h + 256]
            ).astype(BF16)
            remote(out.at[:, cols], out.at[:, cols], so, ro, 1 - s, me)
    landed(xr.at[pl.ds(0, 64)], ro)
    landed(xr.at[pl.ds(0, 64)], so)
    landed(xr.at[pl.ds(0, 1008)], ss)
    landed(xr, sx)
    landed(yrecv, sy)
    landed(back.at[pl.ds(0, 1008)], sb)


def experts(mixed, gain, router_t, ids_t, gate, up, down):
    sems = pltpu.SemaphoreType.DMA
    hbm = pl.BlockSpec(memory_space=pl.ANY)
    return pl.pallas_call(
        expert_kernel,
        out_shape=jax.ShapeDtypeStruct((16, 4096), BF16),
        in_specs=[VMEM] * 4 + [hbm] * 3,
        out_specs=VMEM,
        scratch_shapes=[
            pltpu.VMEM((4096, 768), BF16),
            pltpu.VMEM((384, 4096), BF16),
            pltpu.VMEM((16, 4096), BF16),
            pltpu.VMEM((1024, 512), BF16),
            pltpu.VMEM((1024, 512), BF16),
            pltpu.VMEM((256, 4096), BF16),
            pltpu.VMEM((256, 768), F32),
            pltpu.VMEM((256, 384), BF16),
            pltpu.VMEM((8, 256, 256), F32),
            pltpu.VMEM((8, 256, 256), BF16),
            pltpu.VMEM((8, 256, 256), BF16),
            pltpu.VMEM((1024, 512), BF16),
            pltpu.VMEM((1024, 512), BF16),
            pltpu.VMEM((64, 512), BF16),
            sems((3,)), sems, sems((4,)), sems, sems((4,)), sems, sems((8,)), sems, sems,
            sems, sems,
        ],
        compiler_params=pltpu.CompilerParams(
            collective_id=1, has_side_effects=True, vmem_limit_bytes=48 << 20
        ),
        name="experts",
    )(mixed, gain, router_t, ids_t, gate, up, down)


def attend(queries, key_cache, value_cache, new_key, new_value, cache_lengths):
    row_count = queries.shape[0]
    group_count = new_key.shape[1] // HEAD
    per_group = queries.shape[1] // (group_count * HEAD)
    cache_span = key_cache.shape[1]
    score_scale = 1.0 / math.sqrt(HEAD)
    query_heads = queries.reshape(row_count, group_count, per_group, HEAD)
    fresh_keys = new_key.reshape(row_count, group_count, HEAD)
    fresh_values = new_value.reshape(row_count, group_count, HEAD)
    fresh_score = (
        jnp.einsum("rgqh,rgh->rgq", query_heads, fresh_keys, preferred_element_type=jnp.float32)
        * score_scale
    )
    keys_whole = key_cache.reshape(row_count, cache_span, group_count, HEAD)
    scores = (
        jnp.einsum("rgqh,rcgh->rgqc", query_heads, keys_whole, preferred_element_type=jnp.float32)
        * score_scale
    )
    positions = jnp.arange(cache_span, dtype=jnp.int32)
    live_mask = positions[None, :] < cache_lengths[:, None]
    scores = jnp.where(live_mask[:, None, None, :], scores, masked_score)
    row_max = jnp.maximum(jnp.max(scores, axis=-1), fresh_score)
    exp_cache = jnp.exp(scores - row_max[..., None])
    denominator = jnp.sum(exp_cache, axis=-1) + jnp.exp(fresh_score - row_max)
    weights_bf = (exp_cache / denominator[..., None]).astype(jnp.bfloat16)
    values_whole = value_cache.reshape(row_count, cache_span, group_count, HEAD)
    attended = jnp.einsum(
        "rgqc,rcgh->rgqh", weights_bf, values_whole, preferred_element_type=jnp.float32
    )
    fresh_weight = (jnp.exp(fresh_score - row_max) / denominator).astype(jnp.bfloat16)
    attended = (
        attended
        + fresh_weight.astype(jnp.float32)[..., None]
        * fresh_values.astype(jnp.float32)[:, :, None, :]
    )
    return attended.reshape(row_count, group_count * per_group * HEAD).astype(jnp.bfloat16)


def local(
    queries,
    key_cache,
    value_cache,
    new_key,
    new_value,
    cache_lengths,
    residual_in,
    out_weight,
    norm_gain,
    router_weight,
    expert_ids,
    gate_weight,
    up_weight,
    down_weight,
):
    attended = attend(queries, key_cache, value_cache, new_key, new_value, cache_lengths)
    mixed = project(attended, out_weight.T, residual_in)
    return experts(
        mixed,
        norm_gain.reshape(1, -1),
        router_weight.T,
        expert_ids.T,
        gate_weight,
        up_weight,
        down_weight,
    )


def solution(mesh):
    placed = (
        P("dev", "sec"),
        P("dev", None, "sec"),
        P("dev", None, "sec"),
        P("dev", "sec"),
        P("dev", "sec"),
        P("dev"),
        P("dev", None),
        P("sec", "dev"),
        P(),
        P(),
        P("dev", None),
        P("dev", None, "sec"),
        P("dev", None, "sec"),
        P("dev", "sec", None),
    )
    return jax.shard_map(
        local, mesh=mesh, in_specs=placed, out_specs=P("dev", None), check_vma=False
    )
```

```python
import math

import jax
import jax.numpy as jnp
from jax import lax
from jax.experimental import pallas as pl
from jax.experimental.pallas import tpu as pltpu
from jax.sharding import PartitionSpec as P

HEAD = 128
MESH = pl.DeviceIdType.MESH
VMEM = pl.BlockSpec(memory_space=pltpu.VMEM)
F32 = jnp.float32
BF16 = jnp.bfloat16

masked_score = -1e30


def landed(ref, sem):
    pltpu.make_async_copy(ref, ref, sem).wait()


def nt_dot(a, b):
    return lax.dot_general(a, b, (((1,), (1,)), ((), ())), preferred_element_type=F32)


def tn_dot(a, b):
    return lax.dot_general(a, b, (((0,), (0,)), ((), ())), preferred_element_type=F32)


def greet(s, me, n_dev):
    barrier = pltpu.get_barrier_semaphore()
    pl.semaphore_signal(barrier, inc=1, device_id=(1 - s, me), device_id_type=MESH)

    def body(i, carry):
        pl.semaphore_signal(
            barrier, inc=1, device_id=(s, lax.rem(me + i, n_dev)), device_id_type=MESH
        )
        return carry

    lax.fori_loop(1, n_dev, body, 0)


def met(n_dev):
    pl.semaphore_wait(pltpu.get_barrier_semaphore(), n_dev)


def remote(src, dst, send_sem, recv_sem, s, d):
    pltpu.make_async_remote_copy(
        src_ref=src,
        dst_ref=dst,
        send_sem=send_sem,
        recv_sem=recv_sem,
        device_id=(s, d),
        device_id_type=MESH,
    ).start()


ORDER = (2, 1, 3, 0)


def layer_kernel(
    lengths, queries, new_key, new_value, gain, ids_t,
    keys, values, wt, residual, router_t, gate, up, down,
    out,
    kbuf, vbuf, qf, nkf, nvf, attf, att, wbuf, abuf, pown, psend, precv, rsend, rbuf,
    res, rout, mixed, wgu, wd, normed, stack, sbuf, xr, x, act, hid, yown, ysend, yrecv,
    rs, back,
    kv, lw, sw, rw, sa, ra, sx, rx, sr, rr, sm, rm,
    sd, rd, se, re, sy, ry, sb, rb, so, ro,
):
    n_dev = 64
    s = lax.axis_index("sec")
    me = lax.axis_index("dev")
    group, part = me // 8, lax.rem(me, 8)
    mz, mx, my = me // 16, lax.rem(me // 4, 4), lax.rem(me, 4)
    sigma = mz + mx + my

    def own(j):
        return pl.ds(pl.multiple_of(512 * j + 256 * s, 256), 256)

    def other(j):
        return pl.ds(pl.multiple_of(512 * j + 256 * (1 - s), 256), 256)

    def tile16(i):
        return pl.ds(pl.multiple_of(i * 16, 16), 16)

    def peer(i, shift):
        z = lax.rem(mz + 2 + 3 * (i // 4), 4)
        c = lax.rem(mx + 2 + 3 * lax.rem(i, 4), 4)
        y = lax.rem(sigma + shift + 16 - z - c, 4)
        return 16 * z + 4 * c + y

    greet(s, me, n_dev)
    for g in range(4):
        rows = pl.ds(4 * g, 4)
        pltpu.make_async_copy(keys.at[rows], kbuf.at[rows], kv.at[2 * g]).start()
        pltpu.make_async_copy(values.at[rows], vbuf.at[rows], kv.at[2 * g + 1]).start()
    pltpu.make_async_copy(
        wt.at[:, pl.ds(pl.multiple_of(part * 512, 512), 512)],
        wbuf.at[pl.ds(pl.multiple_of(part * 64, 64), 64)],
        rw,
    ).start()
    loads = [
        pltpu.make_async_copy(residual, res, lw.at[0]),
        pltpu.make_async_copy(router_t, rout, lw.at[1]),
        pltpu.make_async_copy(gate.at[0], wgu.at[:, pl.ds(0, 384)], lw.at[2]),
        pltpu.make_async_copy(up.at[0], wgu.at[:, pl.ds(384, 384)], lw.at[3]),
        pltpu.make_async_copy(down.at[0], wd, lw.at[4]),
    ]
    for load in loads:
        load.start()

    for h in range(32):
        qf[pl.ds(16 * h, 16), :] = queries[:, pl.ds(128 * h, 128)].astype(F32)
    nkf[...] = new_key[...].astype(F32)
    nvf[...] = new_value[...].astype(F32)
    scale = 1.0 / math.sqrt(HEAD)
    slot = lax.broadcasted_iota(jnp.int32, (32, 768), 1)
    first_group = lax.broadcasted_iota(jnp.int32, (32, 128), 0) < 16

    def attend(g, carry):
        rows = pl.ds(4 * g, 4)
        landed(kbuf.at[rows], kv.at[2 * g])
        landed(vbuf.at[rows], kv.at[2 * g + 1])
        for u in range(4):
            r = 4 * g + u
            heads = qf[pl.ds(r, 32, stride=16), :]
            wide = jnp.concatenate(
                [jnp.where(first_group, heads, 0.0), jnp.where(first_group, 0.0, heads)], axis=1
            )
            scores = nt_dot(wide.astype(BF16), kbuf[r]) * scale
            scores = jnp.where(slot < lengths[r], scores, masked_score)
            fresh = jnp.sum(wide * nkf[pl.ds(r, 1), :], axis=-1, keepdims=True) * scale
            top = jnp.maximum(jnp.max(scores, axis=-1, keepdims=True), fresh)
            raised = jnp.exp(scores - top)
            raised_fresh = jnp.exp(fresh - top)
            inverse = 1.0 / (jnp.sum(raised, axis=-1, keepdims=True) + raised_fresh)
            probs = (raised * inverse).astype(BF16)
            fresh_prob = (raised_fresh * inverse).astype(BF16).astype(F32)
            result = jnp.dot(probs, vbuf[r], preferred_element_type=F32)
            result += fresh_prob * nvf[pl.ds(r, 1), :]
            attf[pl.ds(r, 32, stride=16), :] = jnp.where(
                first_group, result[:, :128], result[:, 128:]
            )

        @pl.when(g == 1)
        def _():
            met(n_dev)

            def send_w(i, inner):
                m = lax.rem(part + i, 8)
                remote(
                    wt.at[:, pl.ds(pl.multiple_of(m * 512, 512), 512)],
                    wbuf.at[pl.ds(pl.multiple_of(part * 64, 64), 64)],
                    sw, rw, s, group * 8 + m,
                )
                return inner

            lax.fori_loop(1, 8, send_w, 0)

        return carry

    lax.fori_loop(0, 4, attend, 0)
    att[...] = attf[...].astype(BF16)

    def send_class(c, at, slots, block, send_sem, recv_sem):
        def body(i, carry):
            d = peer(i, -c)
            src = at(d)
            dst = slots.at[
                pl.ds(pl.multiple_of((16 * c + me // 4) * block, block), block)
            ]
            if c == 0:

                @pl.when(d != me)
                def _():
                    remote(src, dst, send_sem, recv_sem.at[c], s, d)

                @pl.when(d == me)
                def _():
                    pltpu.make_async_copy(src, dst, recv_sem.at[c]).start()
            else:
                remote(src, dst, send_sem, recv_sem.at[c], s, d)
            return carry

        lax.fori_loop(0, 16, body, 0)

    def return_class(c, at, slots, send_sem, recv_sem):
        def body(i, carry):
            d = peer(i, c)
            src = at(d)
            dst = slots.at[tile16(me)]
            if c == 0:

                @pl.when(d != me)
                def _():
                    remote(src, dst, send_sem, recv_sem, s, d)

                @pl.when(d == me)
                def _():
                    pltpu.make_async_copy(src, dst, recv_sem).start()
            else:
                remote(src, dst, send_sem, recv_sem, s, d)
            return carry

        lax.fori_loop(0, 16, body, 0)

    for c in ORDER:
        send_class(
            c,
            lambda d: att.at[pl.ds(pl.multiple_of(lax.rem(d, 8) * 64, 64), 64)],
            abuf, 64, sa, ra,
        )
    landed(wbuf, rw)
    own_cols = pl.ds(pl.multiple_of(s * 256, 256), 256)
    other_cols = pl.ds(pl.multiple_of((1 - s) * 256, 256), 256)
    for c in ORDER:
        landed(abuf.at[pl.ds(1024 * c, 1024)], ra.at[c])
        rows = pl.ds(256 * c, 256)
        a = jnp.concatenate(
            [
                jnp.concatenate(
                    [abuf[pl.ds(1024 * c + 64 * i + 16 * h, 16), :] for h in range(4)], axis=1
                )
                for i in range(16)
            ],
            axis=0,
        )
        psend[rows] = nt_dot(a, wbuf[other_cols]).astype(BF16)
        remote(psend.at[rows], precv.at[rows], sx, rx.at[c], 1 - s, me)
        pown[rows] = nt_dot(a, wbuf[own_cols])
        landed(precv.at[rows], rx.at[c])
        rsend[rows] = (pown[rows] + precv[rows].astype(F32)).astype(BF16)
        return_class(c, lambda d: rsend.at[tile16(16 * c + d // 4)], rbuf, sr, rr)

    chosen_t = jnp.zeros((64, 16), F32)
    expert_row = lax.broadcasted_iota(jnp.int32, (64, 16), 0)
    for k in range(8):
        chosen_t += jnp.where(ids_t[pl.ds(k, 1), :] == expert_row, 1.0, 0.0)
    earlier = jnp.where(
        lax.broadcasted_iota(jnp.int32, (16, 16), 0) < lax.broadcasted_iota(jnp.int32, (16, 16), 1),
        1.0,
        0.0,
    ).astype(BF16)
    chosen_tb = chosen_t.astype(BF16)
    rank_tb = jnp.dot(chosen_tb, earlier, preferred_element_type=F32).astype(BF16)
    lane = lax.broadcasted_iota(jnp.int32, (64, 1024), 1)
    spread = jnp.where(
        lane // 16 == lax.broadcasted_iota(jnp.int32, (64, 1024), 0), 1.0, 0.0
    ).astype(BF16)
    chosen_x = tn_dot(chosen_tb, spread)
    rank_x = tn_dot(rank_tb, spread)
    lane16 = lax.broadcasted_iota(jnp.int32, (16, 1024), 1)
    slot_hot = jnp.where(rank_x == lax.rem(lane16, 4).astype(F32), chosen_x, 0.0)
    quarter = lax.rem(lane16 // 4, 4)
    placed = jnp.concatenate(
        [jnp.where(quarter == q, slot_hot, 0.0) for q in range(4)], axis=0
    )
    eye = jnp.where(
        lax.broadcasted_iota(jnp.int32, (64, 64), 0) == lax.broadcasted_iota(jnp.int32, (64, 64), 1),
        1.0,
        0.0,
    ).astype(BF16)
    chosen = tn_dot(chosen_tb, eye)
    row = lax.broadcasted_iota(jnp.int32, (256, 256), 0)
    col = lax.broadcasted_iota(jnp.int32, (256, 256), 1)
    source = (lax.rem(row, 64) // 4) * 16 + (row // 64) * 4 + lax.rem(row, 4)
    order = jnp.where(col == source, 1.0, 0.0).astype(BF16)

    loads[0].wait()
    landed(rbuf, rr)
    for j in range(8):
        total = rbuf[pl.ds(128 * j, 16)].astype(F32)
        for k in range(1, 8):
            total += rbuf[pl.ds(128 * j + 16 * k, 16)].astype(F32)
        cols = own(j)
        mixed[:, cols] = (
            res[:, cols].astype(F32) + total.astype(BF16).astype(F32)
        ).astype(BF16)
        remote(mixed.at[:, cols], mixed.at[:, cols], sm, rm, 1 - s, me)
    landed(mixed.at[:, pl.ds(0, 2048)], rm)

    mixed_f = mixed[...].astype(F32)
    mean_square = jnp.mean(mixed_f * mixed_f, axis=-1, keepdims=True)
    normed[...] = (mixed_f * lax.rsqrt(mean_square + 1e-06) * gain[...]).astype(BF16)
    for q in range(4):
        stack[pl.ds(16 * q, 16), pl.ds(0, 256)] = normed[:, own(2 * q)]
        stack[pl.ds(16 * q, 16), pl.ds(256, 256)] = normed[:, own(2 * q + 1)]
    sbuf[...] = tn_dot(placed.astype(BF16), stack[...]).astype(BF16)
    for c in ORDER:
        send_class(c, lambda d: sbuf.at[tile16(d)], xr, 16, sd, rd)

    loads[1].wait()
    logits = nt_dot(normed[...], rout[...])
    masked = jnp.where(chosen > 0.5, logits, masked_score)
    top = jnp.max(masked, axis=-1, keepdims=True)
    raised = jnp.where(chosen > 0.5, jnp.exp(masked - top), 0.0)
    weights = raised / jnp.sum(raised, axis=-1, keepdims=True)
    high = weights.astype(BF16)
    low = (weights - high.astype(F32)).astype(BF16)
    high_x = jnp.dot(high, spread, preferred_element_type=F32)
    low_x = jnp.dot(low, spread, preferred_element_type=F32)
    combine_high = (placed * jnp.concatenate([high_x] * 4, axis=0)).astype(BF16)
    combine_low = (placed * jnp.concatenate([low_x] * 4, axis=0)).astype(BF16)
    for load in loads[2:]:
        load.wait()

    for half in range(2):
        mine = pl.ds(128 * half, 128)
        for t in range(2):
            c = ORDER[2 * half + t]
            rows = pl.ds(128 * half + 64 * t, 64)
            landed(xr.at[pl.ds(256 * c, 256)], rd.at[c])
            y = jnp.dot(order, xr[pl.ds(256 * c, 256)], preferred_element_type=F32).astype(BF16)
            for q in range(4):
                x[rows, own(2 * q)] = y[64 * q : 64 * q + 64, :256]
                x[rows, own(2 * q + 1)] = y[64 * q : 64 * q + 64, 256:]
            for j in range(8):
                remote(x.at[rows, own(j)], x.at[rows, own(j)], se, re.at[half], 1 - s, me)
        landed(x.at[mine, pl.ds(0, 2048)], re.at[half])

        def gate_up(n, carry):
            cols = pl.ds(pl.multiple_of(n * 256, 256), 256)
            act[:, cols] = jnp.dot(x[mine], wgu[:, cols], preferred_element_type=F32)
            return carry

        lax.fori_loop(0, 3, gate_up, 0)
        gated = act[:, pl.ds(0, 384)]
        hid[...] = (gated / (1.0 + jnp.exp(-gated)) * act[:, pl.ds(384, 384)]).astype(BF16)

        def down_other(j, carry):
            ysend[half, j] = jnp.dot(
                hid[...], wd[:, other(j)], preferred_element_type=F32
            ).astype(BF16)
            remote(ysend.at[half, j], yrecv.at[half, j], sy, ry.at[half], 1 - s, me)
            return carry

        lax.fori_loop(0, 8, down_other, 0)

        def down_own(j, carry):
            yown[j] = jnp.dot(hid[...], wd[:, own(j)], preferred_element_type=F32)
            return carry

        lax.fori_loop(0, 8, down_own, 0)
        landed(yrecv.at[half], ry.at[half])
        for t in range(2):
            c = ORDER[2 * half + t]
            rows = pl.ds(64 * t, 64)
            parts = [
                jnp.concatenate(
                    [
                        (yown[j, rows] + yrecv[half, j, rows].astype(F32)).astype(BF16)
                        for j in (2 * q, 2 * q + 1)
                    ],
                    axis=1,
                )
                for q in range(4)
            ]
            rs[pl.ds(256 * c, 256)] = tn_dot(order, jnp.concatenate(parts, axis=0)).astype(BF16)
            return_class(c, lambda d: rs.at[tile16(16 * c + d // 4)], back, sb, rb)

    landed(back, rb)
    summed = jnp.dot(combine_high, back[...], preferred_element_type=F32)
    summed += jnp.dot(combine_low, back[...], preferred_element_type=F32)
    for q in range(4):
        for h in range(2):
            cols = own(2 * q + h)
            out[:, cols] = (
                mixed[:, cols].astype(F32)
                + summed[16 * q : 16 * q + 16, 256 * h : 256 * h + 256]
            ).astype(BF16)
            remote(out.at[:, cols], out.at[:, cols], so, ro, 1 - s, me)
    landed(wbuf.at[pl.ds(0, 448)], sw)
    landed(abuf.at[pl.ds(0, 4032)], sa)
    landed(psend, sx)
    landed(rbuf.at[pl.ds(0, 1008)], sr)
    landed(mixed.at[:, pl.ds(0, 2048)], sm)
    landed(xr.at[pl.ds(0, 1008)], sd)
    landed(x.at[:, pl.ds(0, 2048)], se)
    landed(yrecv, sy)
    landed(back.at[pl.ds(0, 1008)], sb)
    landed(mixed.at[:, pl.ds(0, 2048)], so)
    landed(out.at[:, pl.ds(0, 2048)], ro)


def local(
    queries,
    key_cache,
    value_cache,
    new_key,
    new_value,
    cache_lengths,
    residual_in,
    out_weight,
    norm_gain,
    router_weight,
    expert_ids,
    gate_weight,
    up_weight,
    down_weight,
):
    sems = pltpu.SemaphoreType.DMA
    hbm = pl.BlockSpec(memory_space=pl.ANY)
    return pl.pallas_call(
        layer_kernel,
        out_shape=jax.ShapeDtypeStruct((16, 4096), BF16),
        in_specs=[pl.BlockSpec(memory_space=pltpu.SMEM)] + [VMEM] * 5 + [hbm] * 8,
        out_specs=VMEM,
        scratch_shapes=[
            pltpu.VMEM((16, 768, 256), BF16),
            pltpu.VMEM((16, 768, 256), BF16),
            pltpu.VMEM((512, 128), F32),
            pltpu.VMEM((16, 256), F32),
            pltpu.VMEM((16, 256), F32),
            pltpu.VMEM((512, 128), F32),
            pltpu.VMEM((512, 128), BF16),
            pltpu.VMEM((512, 512), BF16),
            pltpu.VMEM((4096, 128), BF16),
            pltpu.VMEM((1024, 256), F32),
            pltpu.VMEM((1024, 256), BF16),
            pltpu.VMEM((1024, 256), BF16),
            pltpu.VMEM((1024, 256), BF16),
            pltpu.VMEM((1024, 256), BF16),
            pltpu.VMEM((16, 4096), BF16),
            pltpu.VMEM((64, 4096), BF16),
            pltpu.VMEM((16, 4096), BF16),
            pltpu.VMEM((4096, 768), BF16),
            pltpu.VMEM((384, 4096), BF16),
            pltpu.VMEM((16, 4096), BF16),
            pltpu.VMEM((64, 512), BF16),
            pltpu.VMEM((1024, 512), BF16),
            pltpu.VMEM((1024, 512), BF16),
            pltpu.VMEM((256, 4096), BF16),
            pltpu.VMEM((128, 768), F32),
            pltpu.VMEM((128, 384), BF16),
            pltpu.VMEM((8, 128, 256), F32),
            pltpu.VMEM((2, 8, 128, 256), BF16),
            pltpu.VMEM((2, 8, 128, 256), BF16),
            pltpu.VMEM((1024, 512), BF16),
            pltpu.VMEM((1024, 512), BF16),
            sems((8,)), sems((5,)), sems, sems, sems, sems((4,)), sems, sems((4,)),
            sems, sems, sems, sems,
            sems, sems((4,)), sems, sems((2,)), sems, sems((2,)), sems, sems, sems, sems,
        ],
        compiler_params=pltpu.CompilerParams(
            collective_id=0, has_side_effects=True, vmem_limit_bytes=56 << 20
        ),
        name="layer",
    )(
        cache_lengths,
        queries,
        new_key,
        new_value,
        norm_gain.reshape(1, -1),
        expert_ids.T,
        key_cache,
        value_cache,
        out_weight.T,
        residual_in,
        router_weight.T,
        gate_weight,
        up_weight,
        down_weight,
    )


def solution(mesh):
    placed = (
        P("dev", "sec"),
        P("dev", None, "sec"),
        P("dev", None, "sec"),
        P("dev", "sec"),
        P("dev", "sec"),
        P("dev"),
        P("dev", None),
        P("sec", "dev"),
        P(),
        P(),
        P("dev", None),
        P("dev", None, "sec"),
        P("dev", None, "sec"),
        P("dev", "sec", None),
    )
    return jax.shard_map(
        local, mesh=mesh, in_specs=placed, out_specs=P("dev", None), check_vma=False
    )
```
